1024 devices in a mesh: section: 8 (over z_lo), dp: 16 (over x, z_hi), tensor: 8 (over y, core).
Axes of the slice: x: 4, y: 4, z: 32 (z_hi: 4, z_lo: 8; z = z_hi * 8 + z_lo), core: 2. Of those that a mesh axis runs over, the one named last changes fastest.
Arguments:
- queries: bfloat16 [8, 4096, 8192], P('section', 'dp', 'tensor'), may hold values from -256 to 256
- image: bfloat16 [8192, 2048], P(('section', 'tensor'), 'dp'), may hold values from -6 to 6
- w_key: bfloat16 [8, 8192, 1024], P('section', None, 'tensor'), may hold values from -0.0625 to 0.0625
- w_value: bfloat16 [8, 8192, 1024], P('section', None, 'tensor'), may hold values from -0.0625 to 0.0625
- gates: float32 [8], P('section'), may hold values from 0.3 to 1.5
- tiles: int32 [16], P('dp'), may hold values from 1 to 4, as said below
- cotangent: bfloat16 [8, 4096, 8192], P('section', 'dp', 'tensor'), may hold values from -6 to 6
Outputs:
- attended: bfloat16 [8, 4096, 8192], P('section', 'dp', 'tensor')
- d_queries: bfloat16 [8, 4096, 8192], P('section', 'dp', 'tensor')
- d_image: bfloat16 [8192, 2048], P(('section', 'tensor'), 'dp')
The draws below stay inside these ranges and needn't reach their ends.
Inputs may be any that keep to these rules, and one draw needn't show every extreme that they name: The first tiles[b] * 32 image tokens are valid for sample b; some sample has 4 tiles and some has one.
All inputs are finite; a program needn't handle non-finite values.
Results may differ from the reference program's by a relative error of at most 0.013.
The reference program's roundings to bfloat16 on the way (of `key_rows`, `value_rows`, `probs_b`, `d_context`, `d_values`, `d_scores` and `d_keys`) count: a program that leaves them out, or rounds other values in their place, can miss the bound.
Values may be sent and summed in bfloat16 or wider, within the bound.
No kernel may reach another device: no remote copies, remote signals or barrier semaphores. Data moves between devices by JAX's collectives and lax.ppermute only.
A program may use at most 32 MiB of HBM per device.

```python
import math
import jax
import jax.numpy as jnp
from jax import lax

D = 8192
HEADS = 64
KV_HEADS = 8
HD = 128
TILES_MAX = 4
TILE_TOK = 32
TXT = 256
IMG = 128
N_SECTION = 8
N_DP = 16


def draw_tiles(key, part):
    first, second, third = jax.random.split(jax.random.fold_in(key, 11), 3)
    counts = jax.random.randint(first, (N_DP,), 1, TILES_MAX + 1)
    spot_high = jax.random.randint(second, (), 0, N_DP)
    spot_low = (spot_high + 1 + jax.random.randint(third, (), 0, N_DP - 1)) % N_DP
    places = jnp.arange(N_DP)
    counts = jnp.where(places == spot_low, 1, counts)
    counts = jnp.where(places == spot_high, TILES_MAX, counts)
    return counts.astype(jnp.int32)


def draw_queries(key, part):
    first = jax.random.fold_in(jax.random.fold_in(key, 23), 0)
    shape = (N_SECTION, N_DP * TXT, HEADS * HD)
    values = jnp.clip(jax.random.normal(first, shape, jnp.float32), -6.0, 6.0)
    return values.astype(jnp.bfloat16)


def level_of(key, shape, cuts, least, top_value):
    gain, own = 1.0, jax.random.fold_in(key, 6)
    for position, parts in cuts:
        heights = jnp.exp(jax.random.uniform(jax.random.fold_in(own, position), (parts,), jnp.float32, least / len(cuts), top_value / len(cuts)))
        gain = gain * jnp.repeat(heights, shape[position] // parts).reshape([-1 if axis == position else 1 for axis in range(len(shape))])
    return gain


def noise(rng, shape, deviation, bound, shards=(), held_as=jnp.bfloat16):
    array = jax.random.normal(rng, shape, jnp.float32) * deviation
    if len(shards) > 0:
        array = level_of(rng, shape, shards, -0.22, 0.18) * array
    return jnp.clip(array, min=-bound, max=bound).astype(held_as)


def setup_inputs(seed: int = 0) -> dict:
    key_list = jax.random.split(jax.random.key(seed), 8)
    return {
        "queries": draw_queries(jax.random.fold_in(key_list[7], 71), 0),
        "image": noise(key_list[1], (D, N_DP * IMG), 1.0, 6.0, ((0, 64), (1, 16))),
        "w_key": noise(key_list[2], (N_SECTION, D, KV_HEADS * HD), D ** -0.5, 0.0625, ((0, 8), (2, 8))),
        "w_value": noise(key_list[3], (N_SECTION, D, KV_HEADS * HD), D ** -0.5, 0.0625, ((0, 8), (2, 8))),
        "gates": jnp.clip(0.3 + 1.2 * jax.random.uniform(key_list[4], (N_SECTION,), jnp.float32) ** level_of(key_list[4], (N_SECTION,), ((0, 8),), -0.2, 0.2), 0.3, 1.5),
        "tiles": draw_tiles(jax.random.fold_in(key_list[7], 71), 0),
        "cotangent": noise(key_list[6], (N_SECTION, N_DP * TXT, HEADS * HD), 1.0, 6.0, ((0, 8), (1, 16), (2, 8))),
    }


def one_sample(text, features, weight_key, weight_value, gate_value, valid_count, upstream):
    tokens = text.shape[0]
    img_count = features.shape[1]
    width = weight_key.shape[1]
    kv_count = width // HD
    q_count = text.shape[1] // HD
    group = q_count // kv_count
    key_rows = jnp.dot(features.T, weight_key, preferred_element_type=jnp.float32).astype(jnp.bfloat16)
    value_rows = jnp.dot(features.T, weight_value, preferred_element_type=jnp.float32).astype(jnp.bfloat16)
    query_heads = text.astype(jnp.float32).reshape(tokens, kv_count, group, HD)
    key_heads = key_rows.astype(jnp.float32).reshape(img_count, kv_count, HD)
    value_heads = value_rows.astype(jnp.float32).reshape(img_count, kv_count, HD)
    scores = jnp.einsum('tkgd,skd->kgts', query_heads, key_heads) / math.sqrt(HD)
    allowed = jnp.arange(img_count) < valid_count
    scores = jnp.where(allowed, scores, jnp.float32(-1e+30))
    top = lax.optimization_barrier(jnp.max(scores, axis=-1, keepdims=True))
    expo = jnp.exp(scores - top)
    probs = expo / lax.optimization_barrier(jnp.sum(expo, axis=-1, keepdims=True))
    probs_b = probs.astype(jnp.bfloat16).astype(jnp.float32)
    context = jnp.einsum('kgts,skd->tkgd', probs_b, value_heads)
    scale = jnp.tanh(gate_value)
    attended = (scale * context).reshape(tokens, q_count * HD).astype(jnp.bfloat16)
    d_context = (scale * upstream.astype(jnp.float32)).astype(jnp.bfloat16).astype(jnp.float32)
    d_context = d_context.reshape(tokens, kv_count, group, HD)
    d_values = jnp.einsum('kgts,tkgd->skd', probs_b, d_context).astype(jnp.bfloat16)
    d_probs = jnp.einsum('tkgd,skd->kgts', d_context, value_heads)
    delta = lax.optimization_barrier(jnp.sum(probs * d_probs, axis=-1, keepdims=True))
    d_scores = (probs * (d_probs - delta) / math.sqrt(HD)).astype(jnp.bfloat16).astype(jnp.float32)
    d_query = jnp.einsum('kgts,skd->tkgd', d_scores, key_heads).reshape(tokens, q_count * HD).astype(jnp.bfloat16)
    d_keys = jnp.einsum('kgts,tkgd->skd', d_scores, query_heads).astype(jnp.bfloat16)
    d_keys = d_keys.reshape(img_count, width)
    d_values = d_values.reshape(img_count, width)
    term = jnp.dot(weight_key, d_keys.T, preferred_element_type=jnp.float32)
    term = term + jnp.dot(weight_value, d_values.T, preferred_element_type=jnp.float32)
    return (attended, d_query, term)

def reference(queries, image, w_key, w_value, gates, tiles, cotangent):
    n_section = queries.shape[0]
    n_samples = tiles.shape[0]
    width_all = queries.shape[2]
    features = image.reshape(D, n_samples, IMG).transpose(1, 0, 2)
    valid = (tiles * TILE_TOK).astype(jnp.int32)
    attended_all = []
    d_query_all = []
    grad_total = jnp.zeros((n_samples, D, IMG), jnp.float32)
    for section in range(n_section):
        text = queries[section].reshape(n_samples, TXT, width_all)
        upstream = cotangent[section].reshape(n_samples, TXT, width_all)
        runner = jax.vmap(one_sample, in_axes=(0, 0, None, None, None, 0, 0))
        attended, d_query, term = runner(text, features, w_key[section], w_value[section], gates[section], valid, upstream)
        attended_all.append(attended.reshape(n_samples * TXT, width_all))
        d_query_all.append(d_query.reshape(n_samples * TXT, width_all))
        grad_total = grad_total + term
    d_image = grad_total.transpose(1, 0, 2).reshape(D, n_samples * IMG).astype(jnp.bfloat16)
    return (jnp.stack(attended_all), jnp.stack(d_query_all), d_image)
```

```python
import math

import jax
import jax.numpy as jnp
from jax import lax
from jax.experimental import pallas as pl
from jax.experimental.pallas import tpu as pltpu
from jax.sharding import PartitionSpec as P

HD = 128
TILE_TOK = 32
IMG = 128
BLK = 128
N_SEC = 8
N_TEN = 8
GROUP = 8
TXT = 256
VMEM_GRANT = 16 << 20
VMEM_GRANT = 16 << 20

F32 = jnp.float32
BF16 = jnp.bfloat16


NN = (((1,), (0,)), ((), ()))
NT = (((1,), (1,)), ((), ()))
TN = (((0,), (0,)), ((), ()))


def dot(a, b, dims):
    return lax.dot_general(a, b, dims, preferred_element_type=F32)


def blocks(t_ref):
    t = t_ref[0]
    step = 2 - 4 * (((t >> 1) + t) & 1)
    own = [t, (t + step) % N_TEN, (t - step) % N_TEN, (t + 4) % N_TEN]
    return own, [own[0] ^ 1, own[2] ^ 1, own[1] ^ 1, own[3] ^ 1]


def project(img_ref, wk_ref, wv_ref, picks):
    total = None
    for n, pick in enumerate(picks):
        for j in range(0, N_SEC, 2):
            left = jnp.concatenate([img_ref[n, j], img_ref[n, j + 1]], axis=1)
            keys = wk_ref[j : j + 2, pick].reshape(2 * BLK, HD)
            values = wv_ref[j : j + 2, pick].reshape(2 * BLK, HD)
            part = dot(left, jnp.concatenate([keys, values], axis=1), NN)
            total = part if total is None else total + part
    return total


def project_kernel(t_ref, own_ref, other_ref, wk_ref, wv_ref, out_ref):
    own, other = blocks(t_ref)
    out_ref[...] = project(own_ref, wk_ref, wv_ref, own[:2]) + project(other_ref, wk_ref, wv_ref, other[:2])


def term(wk_ref, wv_ref, grads, pick):
    weights = jnp.concatenate(
        [wk_ref[:, pick].reshape(N_SEC * BLK, HD), wv_ref[:, pick].reshape(N_SEC * BLK, HD)], axis=1
    )
    return dot(weights, grads, NT).reshape(N_SEC, BLK, IMG)


def attention_kernel(
    t_ref, tiles_ref, gate_ref, part_ref, own_ref, other_ref, wk_ref, wv_ref, q_ref, up_ref,
    probs_ref, dscores_ref, rows_ref, grads_ref, far_ref, near_ref,
):
    own, other = blocks(t_ref)
    rows = part_ref[...] + project(own_ref, wk_ref, wv_ref, own[2:])
    rows = (rows + project(other_ref, wk_ref, wv_ref, other[2:])).astype(BF16)
    rows_ref[...] = rows
    keys = rows[:, :HD]
    values = rows[:, HD:]
    scale = jnp.tanh(jnp.full((1, HD), gate_ref[0], F32))
    limit = tiles_ref[0] * TILE_TOK
    allowed = lax.broadcasted_iota(jnp.int32, (IMG, TXT), 0) < limit
    d_keys = d_values = None
    for h in range(GROUP):
        query = q_ref[:, h * HD : (h + 1) * HD]
        upstream = up_ref[:, h * HD : (h + 1) * HD].astype(F32)
        d_context = (scale * upstream).astype(BF16)
        scores = dot(keys, query, NT) * F32(1.0 / math.sqrt(HD))
        scores = jnp.where(allowed, scores, F32(-1e30))
        top = jnp.max(scores, axis=0, keepdims=True)
        expo = jnp.exp(scores - top)
        probs = expo * (1.0 / jnp.sum(expo, axis=0, keepdims=True))
        probs_b = probs.astype(BF16)
        probs_ref[h] = probs_b
        d_probs = dot(values, d_context, NT)
        delta = jnp.sum(probs * d_probs, axis=0, keepdims=True)
        d_scores = (probs * (d_probs - delta) * F32(1.0 / math.sqrt(HD))).astype(BF16)
        dscores_ref[h] = d_scores
        dv = dot(probs_b, d_context, NN)
        dk = dot(d_scores, query, NN)
        d_values = dv if d_values is None else d_values + dv
        d_keys = dk if d_keys is None else d_keys + dk
    grads = jnp.concatenate([d_keys.astype(BF16), d_values.astype(BF16)], axis=1)
    grads_ref[...] = grads
    for n in range(2):
        far_ref[n] = term(wk_ref, wv_ref, grads, other[2 + n]).astype(BF16)
        near_ref[n] = term(wk_ref, wv_ref, grads, other[n]).astype(BF16)


def join_kernel(keep_ref, second_ref, first_ref, out_ref):
    total = keep_ref[...] + second_ref[0].astype(F32) + first_ref[...].astype(F32)
    out_ref[...] = total.astype(BF16)


def term_far_kernel(t_ref, wk_ref, wv_ref, grads_ref, in_ref, out_ref):
    own, _ = blocks(t_ref)
    grads = grads_ref[...]
    out_ref[0] = (term(wk_ref, wv_ref, grads, own[2]) + in_ref[0].astype(F32)).astype(BF16)
    out_ref[1] = (term(wk_ref, wv_ref, grads, own[3]) + in_ref[1].astype(F32)).astype(BF16)


def term_near_kernel(t_ref, wk_ref, wv_ref, grads_ref, in_ref, out0_ref, out1_ref):
    own, _ = blocks(t_ref)
    grads = grads_ref[...]
    out0_ref[...] = term(wk_ref, wv_ref, grads, own[0]) + in_ref[0].astype(F32)
    out1_ref[...] = term(wk_ref, wv_ref, grads, own[1]) + in_ref[1].astype(F32)


def attended_kernel(gate_ref, probs_ref, rows_ref, out_ref):
    values = rows_ref[:, HD:]
    scale = jnp.tanh(jnp.full((1, HD), gate_ref[0], F32))
    for h in range(GROUP):
        context = dot(probs_ref[h], values, TN)
        out_ref[:, h * HD : (h + 1) * HD] = (scale * context).astype(BF16)


def dquery_kernel(dscores_ref, rows_ref, out_ref):
    keys = rows_ref[:, :HD]
    for h in range(GROUP):
        out_ref[:, h * HD : (h + 1) * HD] = dot(dscores_ref[h], keys, TN).astype(BF16)


def call(kernel, name, outs, flops, *args):
    smem = pl.BlockSpec(memory_space=pltpu.SMEM)
    vmem = pl.BlockSpec(memory_space=pltpu.VMEM)
    return pl.pallas_call(
        kernel,
        name=name,
        out_shape=outs,
        in_specs=[smem if a.ndim == 1 else vmem for a in args],
        out_specs=jax.tree.map(lambda _: vmem, outs),
        cost_estimate=pl.CostEstimate(flops=flops, transcendentals=0, bytes_accessed=1 << 20),
        compiler_params=pltpu.CompilerParams(vmem_limit_bytes=VMEM_GRANT),
    )(*[a if a.ndim == 1 else pltpu.with_memory_space_constraint(a, pltpu.VMEM) for a in args])


def arr(dtype, *shape):
    return pltpu.VMEM(shape, dtype)


def load_kernel(*refs):
    count = len(refs) // 3
    copies = [pltpu.make_async_copy(refs[n], refs[count + n], refs[2 * count + n]) for n in range(count)]
    for copy in copies:
        copy.start()
    for copy in copies:
        copy.wait()


def load(*args):
    return pl.pallas_call(
        load_kernel,
        name="load",
        out_shape=tuple(arr(a.dtype, *a.shape) for a in args),
        in_specs=[pl.BlockSpec(memory_space=pltpu.HBM) for _ in args],
        out_specs=tuple(pl.BlockSpec(memory_space=pltpu.VMEM) for _ in args),
        scratch_shapes=[pltpu.SemaphoreType.DMA for _ in args],
        cost_estimate=pl.CostEstimate(flops=0, transcendentals=0, bytes_accessed=10 << 20),
        compiler_params=pltpu.CompilerParams(vmem_limit_bytes=VMEM_GRANT),
    )(*[pltpu.with_memory_space_constraint(a, pltpu.HBM) for a in args])


def shards(queries, image, w_key, w_value, gates, tiles, cotangent):
    wk = w_key.reshape(N_SEC, N_TEN, BLK, HD)
    wv = w_value.reshape(N_SEC, N_TEN, BLK, HD)
    text = queries[0]
    upstream = cotangent[0]
    me = lax.axis_index("tensor").astype(jnp.int32).reshape(1)

    def turn(t):
        return 2 - 4 * (((t >> 1) + t) & 1)

    partner = [(t, t ^ 1) for t in range(N_TEN)]
    first = [(t, (t + turn(t)) % N_TEN) for t in range(N_TEN)]
    second = [(t, (t - turn(t)) % N_TEN) for t in range(N_TEN)]

    def send(x, perm, name):
        with jax.named_scope(name):
            return lax.ppermute(x, "tensor", perm)

    image, me, gates, tiles = lax.optimization_barrier((image, me, gates, tiles))
    flat = jnp.broadcast_to(image.T[None], (N_SEC, IMG, BLK))
    mine = lax.all_to_all(flat, "section", 0, 0)
    wk, wv, text, upstream, mine = lax.optimization_barrier((wk, wv, text, upstream, mine))
    wk, wv, text, upstream = load(wk, wv, text, upstream)
    got = send(mine, first, "ag_first")
    got, wk, wv, text, upstream = lax.optimization_barrier((got, wk, wv, text, upstream))
    near = jnp.stack([mine, got])
    far = send(near, second, "ag_second")
    other_near = send(near, partner, "ag_partner_near")
    part = call(project_kernel, "project", arr(F32, IMG, 2 * HD), 1 << 29, me, near, other_near, wk, wv)
    other_far = send(far, partner, "ag_partner_far")

    probs, d_scores, rows, grads, out_far, out_near = call(
        attention_kernel, "attention",
        (
            arr(BF16, GROUP, IMG, TXT), arr(BF16, GROUP, IMG, TXT),
            arr(BF16, IMG, 2 * HD), arr(BF16, IMG, 2 * HD),
            arr(BF16, 2, N_SEC, BLK, IMG), arr(BF16, 2, N_SEC, BLK, IMG),
        ),
        1 << 30, me, tiles, gates, part, far, other_far, wk, wv, text, upstream,
    )
    in_far = send(out_far, partner, "rs_partner_far")
    to_second = call(
        term_far_kernel, "term_far", arr(BF16, 2, N_SEC, BLK, IMG), 1 << 28, me, wk, wv, grads, in_far
    )
    to_second, out_near = lax.optimization_barrier((to_second, out_near))
    got_second = send(to_second, second, "rs_second")
    in_near = send(out_near, partner, "rs_partner_near")
    keep, pass_on = call(
        term_near_kernel, "term_near", (arr(F32, N_SEC, BLK, IMG),) * 2, 1 << 28, me, wk, wv, grads, in_near
    )
    attended = call(
        attended_kernel, "attended", arr(BF16, TXT, GROUP * HD), 1 << 27, gates, probs, rows
    )
    d_query = call(dquery_kernel, "dquery", arr(BF16, TXT, GROUP * HD), 1 << 27, d_scores, rows)
    got_second, attended, d_query = lax.optimization_barrier((got_second, attended, d_query))
    to_first = (pass_on + got_second[1].astype(F32)).astype(BF16)
    got_first = send(to_first, first, "rs_first")
    total = call(join_kernel, "join", arr(BF16, N_SEC, BLK, IMG), 1 << 20, keep, got_second, got_first)
    pieces = lax.all_to_all(total, "section", 0, 0)
    grad = jnp.sum(pieces.astype(F32), axis=0).astype(BF16)
    return (attended[None], d_query[None], grad)


def solution(mesh):
    return jax.shard_map(
        shards,
        mesh=mesh,
        in_specs=(
            P("section", "dp", "tensor"),
            P(("section", "tensor"), "dp"),
            P("section", None, "tensor"),
            P("section", None, "tensor"),
            P("section"),
            P("dp"),
            P("section", "dp", "tensor"),
        ),
        out_specs=(
            P("section", "dp", "tensor"),
            P("section", "dp", "tensor"),
            P(("section", "tensor"), "dp"),
        ),
        check_vma=False,
    )
```

```python
import functools
import math

import jax
import jax.numpy as jnp
from jax import lax
from jax.experimental import pallas as pl
from jax.experimental.pallas import tpu as pltpu
from jax.sharding import PartitionSpec as P


HD = 128
TILE_TOK = 32
IMG = 128
BLK = 128
N_SEC = 8
N_TEN = 8
N_HALF = 4
GROUP = 8
TXT = 256
VMEM_GRANT = 16 << 20
VMEM_GRANT = 16 << 20

F32 = jnp.float32
BF16 = jnp.bfloat16


NN = (((1,), (0,)), ((), ()))
NT = (((1,), (1,)), ((), ()))
TN = (((0,), (0,)), ((), ()))


def dot(a, b, dims):
    return lax.dot_general(a, b, dims, preferred_element_type=F32)


def slots(t):
    step = 2 - 4 * (((t >> 1) + t) & 1)
    return [t, (t + step) % N_TEN, (t - step) % N_TEN, (t + 4) % N_TEN]


def project(total, img_ref, own_ref, peer_ref, base):
    for n in range(2):
        for j in range(0, N_SEC, 2):
            left = jnp.concatenate([img_ref[n, j], img_ref[n, j + 1]], axis=1)
            right = jnp.concatenate(
                [ref[kv, base + n, j : j + 2].reshape(2 * BLK, HD) for ref in (own_ref, peer_ref) for kv in range(2)],
                axis=1,
            )
            part = dot(left, right, NN)
            total = part if total is None else total + part
    return total


def near_kernel(img_ref, own_ref, peer_ref, out_ref):
    out_ref[...] = project(None, img_ref, own_ref, peer_ref, 0)


def far_kernel(part_ref, img_ref, own_ref, peer_ref, out_ref, send_ref):
    total = project(part_ref[...], img_ref, own_ref, peer_ref, 2)
    out_ref[...] = total[:, : 2 * HD]
    send_ref[...] = total[:, 2 * HD :]


def term(own_ref, peer_ref, grads, slot):
    weights = jnp.concatenate(
        [ref[kv, slot].reshape(N_SEC * BLK, HD) for ref in (own_ref, peer_ref) for kv in range(2)], axis=1
    )
    return dot(weights, grads, NT).reshape(N_SEC, BLK, IMG)


def term_kernel(slot, own_ref, peer_ref, grads_ref, others_ref, out_ref):
    grads = jnp.concatenate([grads_ref[...], others_ref[...]], axis=1)
    out_ref[...] = term(own_ref, peer_ref, grads, slot).astype(out_ref.dtype)


def attention_kernel(
    tiles_ref, gate_ref, part_ref, got_ref, q_ref, up_ref, probs_ref, dscores_ref, rows_ref, grads_ref
):
    rows = (part_ref[...] + got_ref[...]).astype(BF16)
    rows_ref[...] = rows
    keys = rows[:, :HD]
    values = rows[:, HD:]
    scale = jnp.tanh(jnp.full((1, HD), gate_ref[0], F32))
    limit = tiles_ref[0] * TILE_TOK
    allowed = lax.broadcasted_iota(jnp.int32, (IMG, TXT), 0) < limit
    d_keys = d_values = None
    for h in range(GROUP):
        query = q_ref[:, h * HD : (h + 1) * HD]
        upstream = up_ref[:, h * HD : (h + 1) * HD].astype(F32)
        d_context = (scale * upstream).astype(BF16)
        scores = dot(keys, query, NT) * F32(1.0 / math.sqrt(HD))
        scores = jnp.where(allowed, scores, F32(-1e30))
        top = jnp.max(scores, axis=0, keepdims=True)
        expo = jnp.exp(scores - top)
        probs = expo * (1.0 / jnp.sum(expo, axis=0, keepdims=True))
        probs_b = probs.astype(BF16)
        probs_ref[h] = probs_b
        d_probs = dot(values, d_context, NT)
        delta = jnp.sum(probs * d_probs, axis=0, keepdims=True)
        d_scores = (probs * (d_probs - delta) * F32(1.0 / math.sqrt(HD))).astype(BF16)
        dscores_ref[h] = d_scores
        dv = dot(probs_b, d_context, NN)
        dk = dot(d_scores, query, NN)
        d_values = dv if d_values is None else d_values + dv
        d_keys = dk if d_keys is None else d_keys + dk
    grads = jnp.concatenate([d_keys.astype(BF16), d_values.astype(BF16)], axis=1)
    grads_ref[...] = grads


def join_kernel(keep_ref, a_ref, b_ref, c_ref, out_ref):
    total = keep_ref[...] + a_ref[...].astype(F32)
    out_ref[...] = (total + b_ref[...].astype(F32) + c_ref[...].astype(F32)).astype(BF16)


def attended_kernel(gate_ref, probs_ref, rows_ref, out_ref):
    values = rows_ref[:, HD:]
    scale = jnp.tanh(jnp.full((1, HD), gate_ref[0], F32))
    for h in range(GROUP):
        context = dot(probs_ref[h], values, TN)
        out_ref[:, h * HD : (h + 1) * HD] = (scale * context).astype(BF16)


def dquery_kernel(dscores_ref, rows_ref, out_ref):
    keys = rows_ref[:, :HD]
    for h in range(GROUP):
        out_ref[:, h * HD : (h + 1) * HD] = dot(dscores_ref[h], keys, TN).astype(BF16)


def arr(dtype, *shape):
    return pltpu.VMEM(shape, dtype)


SMEM_SPEC = pl.BlockSpec(memory_space=pltpu.SMEM)
VMEM_SPEC = pl.BlockSpec(memory_space=pltpu.VMEM)


def call(kernel, outs, flops, *args):
    return pl.pallas_call(
        kernel,
        out_shape=outs,
        in_specs=[SMEM_SPEC if a.ndim == 1 else VMEM_SPEC for a in args],
        out_specs=jax.tree.map(lambda _: VMEM_SPEC, outs),
        cost_estimate=pl.CostEstimate(flops=flops, transcendentals=0, bytes_accessed=1 << 20),
        compiler_params=pltpu.CompilerParams(vmem_limit_bytes=VMEM_GRANT),
    )(*[a if a.ndim == 1 else pltpu.with_memory_space_constraint(a, pltpu.VMEM) for a in args])


def outside(kernel, *args):
    return pl.pallas_call(
        kernel,
        out_shape=jax.ShapeDtypeStruct((TXT, GROUP * HD), BF16),
        in_specs=[SMEM_SPEC if a.ndim == 1 else VMEM_SPEC for a in args],
        out_specs=VMEM_SPEC,
        cost_estimate=pl.CostEstimate(flops=1 << 27, transcendentals=0, bytes_accessed=1 << 20),
        compiler_params=pltpu.CompilerParams(vmem_limit_bytes=VMEM_GRANT),
    )(*[a if a.ndim == 1 else pltpu.with_memory_space_constraint(a, pltpu.VMEM) for a in args])


def run(copies):
    for copy in copies:
        copy.start()
    for copy in copies:
        copy.wait()


def give_kernel(t_ref, wk_ref, wv_ref, out_ref, sem):
    picks = slots(t_ref[0] ^ 1)
    run([
        pltpu.make_async_copy(ref.at[:, pick], out_ref.at[kv, n], sem.at[kv, n])
        for kv, ref in enumerate((wk_ref, wv_ref))
        for n, pick in enumerate(picks)
    ])


def load_kernel(t_ref, wk_ref, wv_ref, q_ref, up_ref, out_ref, q_out, up_out, sem, q_sem, up_sem):
    picks = slots(t_ref[0])
    run([
        pltpu.make_async_copy(ref.at[:, pick], out_ref.at[kv, n], sem.at[kv, n])
        for kv, ref in enumerate((wk_ref, wv_ref))
        for n, pick in enumerate(picks)
    ] + [pltpu.make_async_copy(q_ref, q_out, q_sem), pltpu.make_async_copy(up_ref, up_out, up_sem)])


def load(kernel, outs, sems, place, *args):
    return pl.pallas_call(
        kernel,
        out_shape=outs,
        in_specs=[SMEM_SPEC] + [pl.BlockSpec(memory_space=pltpu.HBM) for _ in args],
        out_specs=jax.tree.map(lambda _: VMEM_SPEC, outs),
        scratch_shapes=sems,
        cost_estimate=pl.CostEstimate(flops=0, transcendentals=0, bytes_accessed=6 << 20),
        compiler_params=pltpu.CompilerParams(vmem_limit_bytes=VMEM_GRANT),
    )(place, *[pltpu.with_memory_space_constraint(a, pltpu.HBM) for a in args])


def shards(queries, image, w_key, w_value, gates, tiles, cotangent):
    wk = w_key.reshape(N_SEC, N_TEN, BLK, HD)
    wv = w_value.reshape(N_SEC, N_TEN, BLK, HD)
    text = queries[0]
    upstream = cotangent[0]
    me = lax.axis_index("tensor").astype(jnp.int32).reshape(1)

    def turn(t):
        return 2 - 4 * (((t >> 1) + t) & 1)

    partner = [(t, t ^ 1) for t in range(N_TEN)]
    first = [(t, (t + turn(t)) % N_TEN) for t in range(N_TEN)]
    second = [(t, (t - turn(t)) % N_TEN) for t in range(N_TEN)]

    def send(x, perm):
        return lax.ppermute(x, "tensor", perm)

    dma = pltpu.SemaphoreType.DMA
    half = arr(BF16, 2, N_HALF, N_SEC, BLK, HD)

    image, me, gates, tiles = lax.optimization_barrier((image, me, gates, tiles))
    flat = jnp.broadcast_to(image.T[None], (N_SEC, IMG, BLK))
    mine = lax.all_to_all(flat, "section", 0, 0)
    wk, wv, text, upstream, mine = lax.optimization_barrier((wk, wv, text, upstream, mine))
    got = send(mine, first)
    give = load(give_kernel, half, [dma((2, N_HALF))], me, wk, wv)
    peer = send(give, partner)
    got, give = lax.optimization_barrier((got, give))
    near = jnp.stack([mine, got])
    wk, wv, text, upstream, near = lax.optimization_barrier((wk, wv, text, upstream, near))
    far = send(near, second)
    own, text, upstream = load(
        load_kernel, (half, arr(BF16, *text.shape), arr(BF16, *upstream.shape)),
        [dma((2, N_HALF)), dma, dma], me, wk, wv, text, upstream,
    )
    part = call(near_kernel, arr(F32, IMG, 4 * HD), 1 << 29, near, own, peer)
    far, part = lax.optimization_barrier((far, part))
    part, out_part = call(far_kernel, (arr(F32, IMG, 2 * HD),) * 2, 1 << 29, part, far, own, peer)
    got_part = send(out_part, partner)

    probs, d_scores, rows, grads = call(
        attention_kernel,
        (arr(BF16, GROUP, IMG, TXT), arr(BF16, GROUP, IMG, TXT), arr(BF16, IMG, 2 * HD), arr(BF16, IMG, 2 * HD)),
        1 << 30, tiles, gates, part, got_part, text, upstream,
    )
    others = send(grads, partner)

    def terms(slot, dtype):
        return call(
            functools.partial(term_kernel, slot), arr(dtype, N_SEC, BLK, IMG), 1 << 28, own, peer, grads, others
        )

    opposite = [(t, (t + 4) % N_TEN) for t in range(N_TEN)]
    got_opposite = send(terms(3, BF16), opposite)
    got_first = send(terms(1, BF16), first)
    got_second = send(terms(2, BF16), second)
    keep = terms(0, F32)
    attended = outside(attended_kernel, gates, probs, rows)
    d_query = outside(dquery_kernel, d_scores, rows)
    keep, attended, d_query = lax.optimization_barrier((keep, attended, d_query))
    total = call(join_kernel, arr(BF16, N_SEC, BLK, IMG), 1 << 20, keep, got_opposite, got_first, got_second)
    pieces = lax.all_to_all(total, "section", 0, 0)
    grad = jnp.sum(pieces.astype(F32), axis=0).astype(BF16)
    return (attended[None], d_query[None], grad)


def solution(mesh):
    return jax.shard_map(
        shards,
        mesh=mesh,
        in_specs=(
            P("section", "dp", "tensor"),
            P(("section", "tensor"), "dp"),
            P("section", None, "tensor"),
            P("section", None, "tensor"),
            P("section"),
            P("dp"),
            P("section", "dp", "tensor"),
        ),
        out_specs=(
            P("section", "dp", "tensor"),
            P("section", "dp", "tensor"),
            P(("section", "tensor"), "dp"),
        ),
        check_vma=False,
    )
```

```python
import functools
import math

import jax
import jax.numpy as jnp
from jax import lax
from jax.experimental import pallas as pl
from jax.experimental.pallas import tpu as pltpu
from jax.sharding import PartitionSpec as P


HD = 128
TILE_TOK = 32
IMG = 128
BLK = 128
N_SEC = 8
N_TEN = 8
N_HALF = 4
GROUP = 8
TXT = 256
VMEM_GRANT = 16 << 20
VMEM_GRANT = 16 << 20

F32 = jnp.float32
BF16 = jnp.bfloat16


NN = (((1,), (0,)), ((), ()))
NT = (((1,), (1,)), ((), ()))
TN = (((0,), (0,)), ((), ()))


def dot(a, b, dims):
    return lax.dot_general(a, b, dims, preferred_element_type=F32)


def slots(t):
    step = 2 - 4 * (((t >> 1) + t) & 1)
    return [t, (t + step) % N_TEN, (t - step) % N_TEN, (t + 4) % N_TEN]


def project_kernel(a_ref, b_ref, c_ref, d_ref, own_ref, peer_ref, out_ref, send_ref):
    total = None
    for slot, img_ref in enumerate((a_ref, b_ref, c_ref, d_ref)):
        for j in range(0, N_SEC, 2):
            left = jnp.concatenate([img_ref[j], img_ref[j + 1]], axis=1)
            right = jnp.concatenate(
                [ref[kv, slot, j : j + 2].reshape(2 * BLK, HD) for ref in (own_ref, peer_ref) for kv in range(2)],
                axis=1,
            )
            part = dot(left, right, NN)
            total = part if total is None else total + part
    out_ref[...] = total[:, : 2 * HD]
    send_ref[...] = total[:, 2 * HD :]


def term(own_ref, peer_ref, grads, slot):
    weights = jnp.concatenate(
        [ref[kv, slot].reshape(N_SEC * BLK, HD) for ref in (own_ref, peer_ref) for kv in range(2)], axis=1
    )
    return dot(weights, grads, NT).reshape(N_SEC, BLK, IMG)


def term_kernel(slot, own_ref, peer_ref, grads_ref, others_ref, out_ref):
    grads = jnp.concatenate([grads_ref[...], others_ref[...]], axis=1)
    out_ref[...] = term(own_ref, peer_ref, grads, slot).astype(out_ref.dtype)


def attention_kernel(
    tiles_ref, gate_ref, part_ref, got_ref, q_ref, up_ref, probs_ref, dscores_ref, rows_ref, grads_ref
):
    rows = (part_ref[...] + got_ref[...]).astype(BF16)
    rows_ref[...] = rows
    keys = rows[:, :HD]
    values = rows[:, HD:]
    scale = jnp.tanh(jnp.full((1, HD), gate_ref[0], F32))
    limit = tiles_ref[0] * TILE_TOK
    allowed = lax.broadcasted_iota(jnp.int32, (IMG, TXT), 0) < limit
    d_keys = d_values = None
    for h in range(GROUP):
        query = q_ref[:, h * HD : (h + 1) * HD]
        upstream = up_ref[:, h * HD : (h + 1) * HD].astype(F32)
        d_context = (scale * upstream).astype(BF16)
        scores = dot(keys, query, NT) * F32(1.0 / math.sqrt(HD))
        scores = jnp.where(allowed, scores, F32(-1e30))
        top = jnp.max(scores, axis=0, keepdims=True)
        expo = jnp.exp(scores - top)
        probs = expo * (1.0 / jnp.sum(expo, axis=0, keepdims=True))
        probs_b = probs.astype(BF16)
        probs_ref[h] = probs_b
        d_probs = dot(values, d_context, NT)
        delta = jnp.sum(probs * d_probs, axis=0, keepdims=True)
        d_scores = (probs * (d_probs - delta) * F32(1.0 / math.sqrt(HD))).astype(BF16)
        dscores_ref[h] = d_scores
        dv = dot(probs_b, d_context, NN)
        dk = dot(d_scores, query, NN)
        d_values = dv if d_values is None else d_values + dv
        d_keys = dk if d_keys is None else d_keys + dk
    grads = jnp.concatenate([d_keys.astype(BF16), d_values.astype(BF16)], axis=1)
    grads_ref[...] = grads


def join_kernel(keep_ref, a_ref, b_ref, c_ref, out_ref):
    total = keep_ref[...] + a_ref[...].astype(F32)
    out_ref[...] = (total + b_ref[...].astype(F32) + c_ref[...].astype(F32)).astype(BF16)


def attended_kernel(gate_ref, probs_ref, rows_ref, out_ref):
    values = rows_ref[:, HD:]
    scale = jnp.tanh(jnp.full((1, HD), gate_ref[0], F32))
    for h in range(GROUP):
        context = dot(probs_ref[h], values, TN)
        out_ref[:, h * HD : (h + 1) * HD] = (scale * context).astype(BF16)


def dquery_kernel(dscores_ref, rows_ref, out_ref):
    keys = rows_ref[:, :HD]
    for h in range(GROUP):
        out_ref[:, h * HD : (h + 1) * HD] = dot(dscores_ref[h], keys, TN).astype(BF16)


def arr(dtype, *shape):
    return pltpu.VMEM(shape, dtype)


SMEM_SPEC = pl.BlockSpec(memory_space=pltpu.SMEM)
VMEM_SPEC = pl.BlockSpec(memory_space=pltpu.VMEM)


def call(kernel, outs, flops, *args):
    return pl.pallas_call(
        kernel,
        out_shape=outs,
        in_specs=[SMEM_SPEC if a.ndim == 1 else VMEM_SPEC for a in args],
        out_specs=jax.tree.map(lambda _: VMEM_SPEC, outs),
        cost_estimate=pl.CostEstimate(flops=flops, transcendentals=0, bytes_accessed=1 << 20),
        compiler_params=pltpu.CompilerParams(vmem_limit_bytes=VMEM_GRANT),
    )(*[a if a.ndim == 1 else pltpu.with_memory_space_constraint(a, pltpu.VMEM) for a in args])


def outside(kernel, *args):
    return pl.pallas_call(
        kernel,
        out_shape=jax.ShapeDtypeStruct((TXT, GROUP * HD), BF16),
        in_specs=[SMEM_SPEC if a.ndim == 1 else VMEM_SPEC for a in args],
        out_specs=VMEM_SPEC,
        cost_estimate=pl.CostEstimate(flops=1 << 27, transcendentals=0, bytes_accessed=1 << 20),
        compiler_params=pltpu.CompilerParams(vmem_limit_bytes=VMEM_GRANT),
    )(*[a if a.ndim == 1 else pltpu.with_memory_space_constraint(a, pltpu.VMEM) for a in args])


def run(copies):
    for copy in copies:
        copy.start()
    for copy in copies:
        copy.wait()


def give_kernel(t_ref, wk_ref, wv_ref, out_ref, sem):
    picks = slots(t_ref[0] ^ 1)
    run([
        pltpu.make_async_copy(ref.at[:, pick], out_ref.at[kv, n], sem.at[kv, n])
        for kv, ref in enumerate((wk_ref, wv_ref))
        for n, pick in enumerate(picks)
    ])


def load_kernel(t_ref, wk_ref, wv_ref, q_ref, up_ref, out_ref, q_out, up_out, sem, q_sem, up_sem):
    picks = slots(t_ref[0])
    run([
        pltpu.make_async_copy(ref.at[:, pick], out_ref.at[kv, n], sem.at[kv, n])
        for kv, ref in enumerate((wk_ref, wv_ref))
        for n, pick in enumerate(picks)
    ] + [pltpu.make_async_copy(q_ref, q_out, q_sem), pltpu.make_async_copy(up_ref, up_out, up_sem)])


def load(kernel, outs, sems, place, *args):
    return pl.pallas_call(
        kernel,
        out_shape=outs,
        in_specs=[SMEM_SPEC] + [pl.BlockSpec(memory_space=pltpu.HBM) for _ in args],
        out_specs=jax.tree.map(lambda _: VMEM_SPEC, outs),
        scratch_shapes=sems,
        cost_estimate=pl.CostEstimate(flops=0, transcendentals=0, bytes_accessed=6 << 20),
        compiler_params=pltpu.CompilerParams(vmem_limit_bytes=VMEM_GRANT),
    )(place, *[pltpu.with_memory_space_constraint(a, pltpu.HBM) for a in args])


def shards(queries, image, w_key, w_value, gates, tiles, cotangent):
    wk = w_key.reshape(N_SEC, N_TEN, BLK, HD)
    wv = w_value.reshape(N_SEC, N_TEN, BLK, HD)
    text = queries[0]
    upstream = cotangent[0]
    me = lax.axis_index("tensor").astype(jnp.int32).reshape(1)

    def turn(t):
        return 2 - 4 * (((t >> 1) + t) & 1)

    partner = [(t, t ^ 1) for t in range(N_TEN)]
    first = [(t, (t + turn(t)) % N_TEN) for t in range(N_TEN)]
    opposite = [(t, (t + 4) % N_TEN) for t in range(N_TEN)]
    second = [(t, (t - turn(t)) % N_TEN) for t in range(N_TEN)]

    def send(x, perm):
        return lax.ppermute(x, "tensor", perm)

    dma = pltpu.SemaphoreType.DMA
    half = arr(BF16, 2, N_HALF, N_SEC, BLK, HD)

    image, me, gates, tiles = lax.optimization_barrier((image, me, gates, tiles))
    flat = jnp.broadcast_to(image.T[None], (N_SEC, IMG, BLK))
    mine = lax.all_to_all(flat, "section", 0, 0)
    wk, wv, text, upstream, mine = lax.optimization_barrier((wk, wv, text, upstream, mine))
    img_opposite = send(mine, opposite)
    img_first = send(mine, first)
    img_second = send(mine, second)
    give = load(give_kernel, half, [dma((2, N_HALF))], me, wk, wv)
    peer = send(give, partner)
    wk, wv, text, upstream, give = lax.optimization_barrier((wk, wv, text, upstream, give))
    own, text, upstream = load(
        load_kernel, (half, arr(BF16, *text.shape), arr(BF16, *upstream.shape)),
        [dma((2, N_HALF)), dma, dma], me, wk, wv, text, upstream,
    )
    part, out_part = call(
        project_kernel, (arr(F32, IMG, 2 * HD),) * 2, 1 << 30,
        mine, img_first, img_second, img_opposite, own, peer,
    )
    got_part = send(out_part, partner)

    probs, d_scores, rows, grads = call(
        attention_kernel,
        (arr(BF16, GROUP, IMG, TXT), arr(BF16, GROUP, IMG, TXT), arr(BF16, IMG, 2 * HD), arr(BF16, IMG, 2 * HD)),
        1 << 30, tiles, gates, part, got_part, text, upstream,
    )
    others = send(grads, partner)

    def terms(slot, dtype):
        return call(
            functools.partial(term_kernel, slot), arr(dtype, N_SEC, BLK, IMG), 1 << 28, own, peer, grads, others
        )

    got_opposite = send(terms(3, BF16), opposite)
    got_first = send(terms(1, BF16), first)
    got_second = send(terms(2, BF16), second)
    keep = terms(0, F32)
    attended = outside(attended_kernel, gates, probs, rows)
    d_query = outside(dquery_kernel, d_scores, rows)
    keep, attended, d_query = lax.optimization_barrier((keep, attended, d_query))
    total = call(join_kernel, arr(BF16, N_SEC, BLK, IMG), 1 << 20, keep, got_opposite, got_first, got_second)
    pieces = lax.all_to_all(total, "section", 0, 0)
    grad = jnp.sum(pieces.astype(F32), axis=0).astype(BF16)
    return (attended[None], d_query[None], grad)


def solution(mesh):
    return jax.shard_map(
        shards,
        mesh=mesh,
        in_specs=(
            P("section", "dp", "tensor"),
            P(("section", "tensor"), "dp"),
            P("section", None, "tensor"),
            P("section", None, "tensor"),
            P("section"),
            P("dp"),
            P("section", "dp", "tensor"),
        ),
        out_specs=(
            P("section", "dp", "tensor"),
            P("section", "dp", "tensor"),
            P(("section", "tensor"), "dp"),
        ),
        check_vma=False,
    )
```

```python
import functools
import math

import jax
import jax.numpy as jnp
from jax import lax
from jax.experimental import pallas as pl
from jax.experimental.pallas import tpu as pltpu
from jax.sharding import PartitionSpec as P


HD = 128
TILE_TOK = 32
IMG = 128
BLK = 128
N_SEC = 8
N_TEN = 8
N_HALF = 4
GROUP = 8
TXT = 256
VMEM_GRANT = 16 << 20
VMEM_GRANT = 16 << 20

F32 = jnp.float32
BF16 = jnp.bfloat16


NN = (((1,), (0,)), ((), ()))
NT = (((1,), (1,)), ((), ()))
TN = (((0,), (0,)), ((), ()))


def dot(a, b, dims):
    return lax.dot_general(a, b, dims, preferred_element_type=F32)


def slots(t):
    step = 2 - 4 * (((t >> 1) + t) & 1)
    return [t, (t + step) % N_TEN, (t - step) % N_TEN, (t + 4) % N_TEN]


def project_kernel(a_ref, b_ref, c_ref, d_ref, own_ref, peer_ref, out_ref, send_ref):
    total = None
    for slot, img_ref in enumerate((a_ref, b_ref, c_ref, d_ref)):
        for j in range(0, N_SEC, 2):
            left = jnp.concatenate([img_ref[j], img_ref[j + 1]], axis=1)
            right = jnp.concatenate(
                [
                    jnp.concatenate([ref[kv, slot, j // 2], ref[kv, slot, j // 2 + N_SEC // 2]], axis=0)
                    for ref in (own_ref, peer_ref)
                    for kv in range(2)
                ],
                axis=1,
            )
            part = dot(left, right, NN)
            total = part if total is None else total + part
    out_ref[...] = total[:, : 2 * HD]
    send_ref[...] = total[:, 2 * HD :]


def term(own_ref, peer_ref, grads, slot):
    weights = jnp.concatenate(
        [ref[kv, slot].reshape(N_SEC * BLK, HD) for ref in (own_ref, peer_ref) for kv in range(2)], axis=1
    )
    return dot(weights, grads, NT).reshape(N_SEC, BLK, IMG)


def term_kernel(slot, own_ref, peer_ref, grads_ref, others_ref, out_ref):
    grads = jnp.concatenate([grads_ref[...], others_ref[...]], axis=1)
    out_ref[...] = term(own_ref, peer_ref, grads, slot).astype(out_ref.dtype)


def attention_kernel(
    tiles_ref, gate_ref, part_ref, got_ref, q_ref, up_ref, probs_ref, dscores_ref, rows_ref, grads_ref
):
    rows = (part_ref[...] + got_ref[...]).astype(BF16)
    rows_ref[...] = rows
    keys = rows[:, :HD]
    values = rows[:, HD:]
    scale = jnp.tanh(jnp.full((1, HD), gate_ref[0], F32))
    limit = tiles_ref[0] * TILE_TOK
    allowed = lax.broadcasted_iota(jnp.int32, (IMG, TXT), 0) < limit
    d_keys = d_values = None
    for h in range(GROUP):
        query = q_ref[:, h * HD : (h + 1) * HD]
        upstream = up_ref[:, h * HD : (h + 1) * HD].astype(F32)
        d_context = (scale * upstream).astype(BF16)
        scores = dot(keys, query, NT) * F32(1.0 / math.sqrt(HD))
        scores = jnp.where(allowed, scores, F32(-1e30))
        top = jnp.max(scores, axis=0, keepdims=True)
        expo = jnp.exp(scores - top)
        probs = expo * (1.0 / jnp.sum(expo, axis=0, keepdims=True))
        probs_b = probs.astype(BF16)
        probs_ref[h] = probs_b
        d_probs = dot(values, d_context, NT)
        delta = jnp.sum(probs * d_probs, axis=0, keepdims=True)
        d_scores = (probs * (d_probs - delta) * F32(1.0 / math.sqrt(HD))).astype(BF16)
        dscores_ref[h] = d_scores
        dv = dot(probs_b, d_context, NN)
        dk = dot(d_scores, query, NN)
        d_values = dv if d_values is None else d_values + dv
        d_keys = dk if d_keys is None else d_keys + dk
    grads = jnp.concatenate([d_keys.astype(BF16), d_values.astype(BF16)], axis=1)
    grads_ref[...] = grads


def join_kernel(keep_ref, a_ref, b_ref, c_ref, out_ref):
    total = keep_ref[...] + a_ref[...].astype(F32)
    total = (total + b_ref[...].astype(F32) + c_ref[...].astype(F32)).astype(BF16)
    for j in range(N_SEC // 2):
        out_ref[j, 0] = total[j]
        out_ref[j, 1] = total[j + N_SEC // 2]


def pair_kernel(layer_ref, own_ref, passed_ref, out_ref):
    upper = jnp.full((BLK, IMG), layer_ref[0], jnp.int32) >= N_SEC // 2
    own = own_ref[...].astype(F32)
    passed = passed_ref[...].astype(F32)
    low = jnp.where(upper, passed, own).T.astype(BF16)
    high = jnp.where(upper, own, passed).T.astype(BF16)
    for n in range(N_SEC // 2):
        out_ref[n, 0] = low
        out_ref[n, 1] = high


def half_kernel(layer_ref, in_ref, keep_ref, send_ref):
    total = in_ref[0].astype(F32)
    for n in range(1, N_SEC // 2):
        total = total + in_ref[n].astype(F32)
    upper = jnp.full((BLK, IMG), layer_ref[0], jnp.int32) >= N_SEC // 2
    keep_ref[...] = jnp.where(upper, total[1], total[0])
    send_ref[...] = jnp.where(upper, total[0], total[1]).astype(BF16)


def attended_kernel(gate_ref, probs_ref, rows_ref, out_ref):
    values = rows_ref[:, HD:]
    scale = jnp.tanh(jnp.full((1, HD), gate_ref[0], F32))
    for h in range(GROUP):
        context = dot(probs_ref[h], values, TN)
        out_ref[:, h * HD : (h + 1) * HD] = (scale * context).astype(BF16)


def dquery_kernel(dscores_ref, rows_ref, out_ref):
    keys = rows_ref[:, :HD]
    for h in range(GROUP):
        out_ref[:, h * HD : (h + 1) * HD] = dot(dscores_ref[h], keys, TN).astype(BF16)


def arr(dtype, *shape):
    return pltpu.VMEM(shape, dtype)


SMEM_SPEC = pl.BlockSpec(memory_space=pltpu.SMEM)
VMEM_SPEC = pl.BlockSpec(memory_space=pltpu.VMEM)


def call(kernel, outs, flops, *args):
    return pl.pallas_call(
        kernel,
        out_shape=outs,
        in_specs=[SMEM_SPEC if a.ndim == 1 else VMEM_SPEC for a in args],
        out_specs=jax.tree.map(lambda _: VMEM_SPEC, outs),
        cost_estimate=pl.CostEstimate(flops=flops, transcendentals=0, bytes_accessed=1 << 20),
        compiler_params=pltpu.CompilerParams(vmem_limit_bytes=VMEM_GRANT),
    )(*[a if a.ndim == 1 else pltpu.with_memory_space_constraint(a, pltpu.VMEM) for a in args])


def outside(kernel, *args):
    return pl.pallas_call(
        kernel,
        out_shape=jax.ShapeDtypeStruct((TXT, GROUP * HD), BF16),
        in_specs=[SMEM_SPEC if a.ndim == 1 else VMEM_SPEC for a in args],
        out_specs=VMEM_SPEC,
        cost_estimate=pl.CostEstimate(flops=1 << 27, transcendentals=0, bytes_accessed=1 << 20),
        compiler_params=pltpu.CompilerParams(vmem_limit_bytes=VMEM_GRANT),
    )(*[a if a.ndim == 1 else pltpu.with_memory_space_constraint(a, pltpu.VMEM) for a in args])


def run(copies):
    for copy in copies:
        copy.start()
    for copy in copies:
        copy.wait()


def give_kernel(t_ref, wk_ref, wv_ref, out_ref, sem):
    picks = slots(t_ref[0] ^ 1)
    run([
        pltpu.make_async_copy(ref.at[:, pick], out_ref.at[kv, n], sem.at[kv, n])
        for kv, ref in enumerate((wk_ref, wv_ref))
        for n, pick in enumerate(picks)
    ])


def load_kernel(t_ref, wk_ref, wv_ref, q_ref, up_ref, out_ref, q_out, up_out, sem, q_sem, up_sem):
    picks = slots(t_ref[0])
    run([
        pltpu.make_async_copy(ref.at[:, pick], out_ref.at[kv, n], sem.at[kv, n])
        for kv, ref in enumerate((wk_ref, wv_ref))
        for n, pick in enumerate(picks)
    ] + [pltpu.make_async_copy(q_ref, q_out, q_sem), pltpu.make_async_copy(up_ref, up_out, up_sem)])


def load(kernel, outs, sems, place, *args):
    return pl.pallas_call(
        kernel,
        out_shape=outs,
        in_specs=[SMEM_SPEC] + [pl.BlockSpec(memory_space=pltpu.HBM) for _ in args],
        out_specs=jax.tree.map(lambda _: VMEM_SPEC, outs),
        scratch_shapes=sems,
        cost_estimate=pl.CostEstimate(flops=0, transcendentals=0, bytes_accessed=6 << 20),
        compiler_params=pltpu.CompilerParams(vmem_limit_bytes=VMEM_GRANT),
    )(place, *[pltpu.with_memory_space_constraint(a, pltpu.HBM) for a in args])


def shards(queries, image, w_key, w_value, gates, tiles, cotangent):
    wk = w_key.reshape(N_SEC, N_TEN, BLK, HD)
    wv = w_value.reshape(N_SEC, N_TEN, BLK, HD)
    text = queries[0]
    upstream = cotangent[0]
    me = lax.axis_index("tensor").astype(jnp.int32).reshape(1)

    def turn(t):
        return 2 - 4 * (((t >> 1) + t) & 1)

    across = [(s, s ^ 4) for s in range(N_SEC)]
    groups = [[0, 1, 2, 3], [4, 5, 6, 7]]
    layer = lax.axis_index("section").astype(jnp.int32).reshape(1)
    partner = [(t, t ^ 1) for t in range(N_TEN)]
    first = [(t, (t + turn(t)) % N_TEN) for t in range(N_TEN)]
    opposite = [(t, (t + 4) % N_TEN) for t in range(N_TEN)]
    second = [(t, (t - turn(t)) % N_TEN) for t in range(N_TEN)]

    def send(x, perm):
        return lax.ppermute(x, "tensor", perm)

    dma = pltpu.SemaphoreType.DMA
    half = arr(BF16, 2, N_HALF, N_SEC, BLK, HD)

    image, me, gates, tiles, layer = lax.optimization_barrier((image, me, gates, tiles, layer))
    passed = lax.ppermute(image, "section", across)
    give = load(give_kernel, half, [dma((2, N_HALF))], me, wk, wv)
    peer = send(give, partner)
    passed, give = lax.optimization_barrier((passed, give))
    flat = pl.pallas_call(
        pair_kernel,
        name="pair",
        out_shape=arr(BF16, N_SEC // 2, 2, IMG, BLK),
        in_specs=[SMEM_SPEC, VMEM_SPEC, VMEM_SPEC],
        out_specs=VMEM_SPEC,
        compiler_params=pltpu.CompilerParams(vmem_limit_bytes=VMEM_GRANT),
    )(layer, image, pltpu.with_memory_space_constraint(passed, pltpu.VMEM))
    mine = lax.all_to_all(flat, "section", 0, 0, axis_index_groups=groups).reshape(N_SEC, IMG, BLK)
    img_opposite = send(mine, opposite)
    img_first = send(mine, first)
    img_second = send(mine, second)
    wk, wv, text, upstream, mine = lax.optimization_barrier((wk, wv, text, upstream, mine))
    own, text, upstream = load(
        load_kernel, (half, arr(BF16, *text.shape), arr(BF16, *upstream.shape)),
        [dma((2, N_HALF)), dma, dma], me, wk, wv, text, upstream,
    )
    part, out_part = call(
        project_kernel, (arr(F32, IMG, 2 * HD),) * 2, 1 << 30,
        mine, img_first, img_second, img_opposite, own, peer,
    )
    got_part = send(out_part, partner)

    probs, d_scores, rows, grads = call(
        attention_kernel,
        (arr(BF16, GROUP, IMG, TXT), arr(BF16, GROUP, IMG, TXT), arr(BF16, IMG, 2 * HD), arr(BF16, IMG, 2 * HD)),
        1 << 30, tiles, gates, part, got_part, text, upstream,
    )
    others = send(grads, partner)

    def terms(slot, dtype):
        return call(
            functools.partial(term_kernel, slot), arr(dtype, N_SEC, BLK, IMG), 1 << 28, own, peer, grads, others
        )

    got_opposite = send(terms(3, BF16), opposite)
    got_first = send(terms(1, BF16), first)
    got_second = send(terms(2, BF16), second)
    keep = terms(0, F32)
    attended = outside(attended_kernel, gates, probs, rows)
    d_query = outside(dquery_kernel, d_scores, rows)
    keep, attended, d_query = lax.optimization_barrier((keep, attended, d_query))
    total = call(join_kernel, arr(BF16, N_SEC // 2, 2, BLK, IMG), 1 << 20, keep, got_opposite, got_first, got_second)
    pieces = lax.all_to_all(total, "section", 0, 0, axis_index_groups=groups)
    stay, leave = call(
        half_kernel, (arr(F32, BLK, IMG), arr(BF16, BLK, IMG)), 1 << 20,
        layer, pieces,
    )
    grad = (stay + lax.ppermute(leave, "section", across).astype(F32)).astype(BF16)
    return (attended[None], d_query[None], grad)


def solution(mesh):
    return jax.shard_map(
        shards,
        mesh=mesh,
        in_specs=(
            P("section", "dp", "tensor"),
            P(("section", "tensor"), "dp"),
            P("section", None, "tensor"),
            P("section", None, "tensor"),
            P("section"),
            P("dp"),
            P("section", "dp", "tensor"),
        ),
        out_specs=(
            P("section", "dp", "tensor"),
            P("section", "dp", "tensor"),
            P(("section", "tensor"), "dp"),
        ),
        check_vma=False,
    )
```

```python
import functools
import math

import jax
import jax.numpy as jnp
from jax import lax
from jax.experimental import pallas as pl
from jax.experimental.pallas import tpu as pltpu
from jax.sharding import PartitionSpec as P


HD = 128
TILE_TOK = 32
IMG = 128
BLK = 128
N_SEC = 8
N_TEN = 8
N_HALF = 4
GROUP = 8
TXT = 256
VMEM_GRANT = 16 << 20
VMEM_GRANT = 16 << 20

F32 = jnp.float32
BF16 = jnp.bfloat16


NN = (((1,), (0,)), ((), ()))
NT = (((1,), (1,)), ((), ()))
TN = (((0,), (0,)), ((), ()))


def dot(a, b, dims):
    return lax.dot_general(a, b, dims, preferred_element_type=F32)


def slots(t):
    step = 2 - 4 * (((t >> 1) + t) & 1)
    return [t, (t + step) % N_TEN, (t - step) % N_TEN, (t + 4) % N_TEN]


def project(total, img_refs, picks, own_ref, peer_ref):
    for slot, img_ref in zip(picks, img_refs):
        for j in range(0, N_SEC, 2):
            left = jnp.concatenate([img_ref[j], img_ref[j + 1]], axis=1)
            right = jnp.concatenate(
                [
                    jnp.concatenate([ref[kv, slot, j // 2], ref[kv, slot, j // 2 + N_SEC // 2]], axis=0)
                    for ref in (own_ref, peer_ref)
                    for kv in range(2)
                ],
                axis=1,
            )
            part = dot(left, right, NN)
            total = part if total is None else total + part
    return total


def project_early_kernel(a_ref, d_ref, own_ref, peer_ref, out_ref):
    out_ref[...] = project(None, (a_ref, d_ref), (0, 3), own_ref, peer_ref)


def project_kernel(part_ref, b_ref, c_ref, own_ref, peer_ref, out_ref, send_ref):
    total = project(part_ref[...], (b_ref, c_ref), (1, 2), own_ref, peer_ref)
    out_ref[...] = total[:, : 2 * HD]
    send_ref[...] = total[:, 2 * HD :]


def term(own_ref, peer_ref, grads, slot):
    weights = jnp.concatenate(
        [ref[kv, slot].reshape(N_SEC * BLK, HD) for ref in (own_ref, peer_ref) for kv in range(2)], axis=1
    )
    return dot(weights, grads, NT).reshape(N_SEC, BLK, IMG)


def term_kernel(slot, own_ref, peer_ref, grads_ref, others_ref, out_ref):
    grads = jnp.concatenate([grads_ref[...], others_ref[...]], axis=1)
    out_ref[...] = term(own_ref, peer_ref, grads, slot).astype(out_ref.dtype)


def attention_kernel(
    tiles_ref, gate_ref, part_ref, got_ref, q_ref, up_ref, probs_ref, dscores_ref, rows_ref, grads_ref
):
    rows = (part_ref[...] + got_ref[...]).astype(BF16)
    rows_ref[...] = rows
    keys = rows[:, :HD]
    values = rows[:, HD:]
    scale = jnp.tanh(jnp.full((1, HD), gate_ref[0], F32))
    limit = tiles_ref[0] * TILE_TOK
    allowed = lax.broadcasted_iota(jnp.int32, (IMG, TXT), 0) < limit
    d_keys = d_values = None
    for h in range(GROUP):
        query = q_ref[:, h * HD : (h + 1) * HD]
        upstream = up_ref[:, h * HD : (h + 1) * HD].astype(F32)
        d_context = (scale * upstream).astype(BF16)
        scores = dot(keys, query, NT) * F32(1.0 / math.sqrt(HD))
        scores = jnp.where(allowed, scores, F32(-1e30))
        top = jnp.max(scores, axis=0, keepdims=True)
        expo = jnp.exp(scores - top)
        probs = expo * (1.0 / jnp.sum(expo, axis=0, keepdims=True))
        probs_b = probs.astype(BF16)
        probs_ref[h] = probs_b
        d_probs = dot(values, d_context, NT)
        delta = jnp.sum(probs * d_probs, axis=0, keepdims=True)
        d_scores = (probs * (d_probs - delta) * F32(1.0 / math.sqrt(HD))).astype(BF16)
        dscores_ref[h] = d_scores
        dv = dot(probs_b, d_context, NN)
        dk = dot(d_scores, query, NN)
        d_values = dv if d_values is None else d_values + dv
        d_keys = dk if d_keys is None else d_keys + dk
    grads = jnp.concatenate([d_keys.astype(BF16), d_values.astype(BF16)], axis=1)
    grads_ref[...] = grads


def term_add_kernel(own_ref, peer_ref, grads_ref, others_ref, in_ref, out_ref):
    grads = jnp.concatenate([grads_ref[...], others_ref[...]], axis=1)
    out_ref[...] = term(own_ref, peer_ref, grads, 0) + in_ref[...].astype(F32)


def join_kernel(keep_ref, b_ref, c_ref, out_ref):
    total = (keep_ref[...] + b_ref[...].astype(F32) + c_ref[...].astype(F32)).astype(BF16)
    for j in range(N_SEC // 2):
        out_ref[j, 0] = total[j]
        out_ref[j, 1] = total[j + N_SEC // 2]


def pair_kernel(layer_ref, own_ref, passed_ref, out_ref):
    upper = jnp.full((BLK, IMG), layer_ref[0], jnp.int32) >= N_SEC // 2
    own = own_ref[...].astype(F32)
    passed = passed_ref[...].astype(F32)
    low = jnp.where(upper, passed, own).T.astype(BF16)
    high = jnp.where(upper, own, passed).T.astype(BF16)
    for n in range(N_SEC // 2):
        out_ref[n, 0] = low
        out_ref[n, 1] = high


def half_kernel(layer_ref, in_ref, keep_ref, send_ref):
    total = in_ref[0].astype(F32)
    for n in range(1, N_SEC // 2):
        total = total + in_ref[n].astype(F32)
    upper = jnp.full((BLK, IMG), layer_ref[0], jnp.int32) >= N_SEC // 2
    keep_ref[...] = jnp.where(upper, total[1], total[0])
    send_ref[...] = jnp.where(upper, total[0], total[1]).astype(BF16)


def attended_kernel(gate_ref, probs_ref, rows_ref, out_ref):
    values = rows_ref[:, HD:]
    scale = jnp.tanh(jnp.full((1, HD), gate_ref[0], F32))
    for h in range(GROUP):
        context = dot(probs_ref[h], values, TN)
        out_ref[:, h * HD : (h + 1) * HD] = (scale * context).astype(BF16)


def dquery_kernel(dscores_ref, rows_ref, out_ref):
    keys = rows_ref[:, :HD]
    for h in range(GROUP):
        out_ref[:, h * HD : (h + 1) * HD] = dot(dscores_ref[h], keys, TN).astype(BF16)


def arr(dtype, *shape):
    return pltpu.VMEM(shape, dtype)


SMEM_SPEC = pl.BlockSpec(memory_space=pltpu.SMEM)
VMEM_SPEC = pl.BlockSpec(memory_space=pltpu.VMEM)


def call(kernel, outs, flops, *args):
    return pl.pallas_call(
        kernel,
        out_shape=outs,
        in_specs=[SMEM_SPEC if a.ndim == 1 else VMEM_SPEC for a in args],
        out_specs=jax.tree.map(lambda _: VMEM_SPEC, outs),
        cost_estimate=pl.CostEstimate(flops=flops, transcendentals=0, bytes_accessed=1 << 20),
        compiler_params=pltpu.CompilerParams(vmem_limit_bytes=VMEM_GRANT),
    )(*[a if a.ndim == 1 else pltpu.with_memory_space_constraint(a, pltpu.VMEM) for a in args])


def outside(kernel, *args):
    return pl.pallas_call(
        kernel,
        out_shape=jax.ShapeDtypeStruct((TXT, GROUP * HD), BF16),
        in_specs=[SMEM_SPEC if a.ndim == 1 else VMEM_SPEC for a in args],
        out_specs=VMEM_SPEC,
        cost_estimate=pl.CostEstimate(flops=1 << 27, transcendentals=0, bytes_accessed=1 << 20),
        compiler_params=pltpu.CompilerParams(vmem_limit_bytes=VMEM_GRANT),
    )(*[a if a.ndim == 1 else pltpu.with_memory_space_constraint(a, pltpu.VMEM) for a in args])


def run(copies):
    for copy in copies:
        copy.start()
    for copy in copies:
        copy.wait()


def give_kernel(t_ref, wk_ref, wv_ref, out_ref, sem):
    picks = slots(t_ref[0] ^ 1)
    run([
        pltpu.make_async_copy(ref.at[:, pick], out_ref.at[kv, n], sem.at[kv, n])
        for kv, ref in enumerate((wk_ref, wv_ref))
        for n, pick in enumerate(picks)
    ])


def load_kernel(t_ref, wk_ref, wv_ref, q_ref, up_ref, out_ref, q_out, up_out, sem, q_sem, up_sem):
    picks = slots(t_ref[0])
    run([
        pltpu.make_async_copy(ref.at[:, pick], out_ref.at[kv, n], sem.at[kv, n])
        for kv, ref in enumerate((wk_ref, wv_ref))
        for n, pick in enumerate(picks)
    ] + [pltpu.make_async_copy(q_ref, q_out, q_sem), pltpu.make_async_copy(up_ref, up_out, up_sem)])


def load(kernel, outs, sems, place, *args):
    return pl.pallas_call(
        kernel,
        out_shape=outs,
        in_specs=[SMEM_SPEC] + [pl.BlockSpec(memory_space=pltpu.HBM) for _ in args],
        out_specs=jax.tree.map(lambda _: VMEM_SPEC, outs),
        scratch_shapes=sems,
        cost_estimate=pl.CostEstimate(flops=0, transcendentals=0, bytes_accessed=6 << 20),
        compiler_params=pltpu.CompilerParams(vmem_limit_bytes=VMEM_GRANT),
    )(place, *[pltpu.with_memory_space_constraint(a, pltpu.HBM) for a in args])


def shards(queries, image, w_key, w_value, gates, tiles, cotangent):
    wk = w_key.reshape(N_SEC, N_TEN, BLK, HD)
    wv = w_value.reshape(N_SEC, N_TEN, BLK, HD)
    text = queries[0]
    upstream = cotangent[0]
    me = lax.axis_index("tensor").astype(jnp.int32).reshape(1)

    def turn(t):
        return 2 - 4 * (((t >> 1) + t) & 1)

    across = [(s, s ^ 4) for s in range(N_SEC)]
    groups = [[0, 1, 2, 3], [4, 5, 6, 7]]
    layer = lax.axis_index("section").astype(jnp.int32).reshape(1)
    partner = [(t, t ^ 1) for t in range(N_TEN)]
    first = [(t, (t + turn(t)) % N_TEN) for t in range(N_TEN)]
    opposite = [(t, (t + 4) % N_TEN) for t in range(N_TEN)]
    second = [(t, (t - turn(t)) % N_TEN) for t in range(N_TEN)]

    def send(x, perm):
        return lax.ppermute(x, "tensor", perm)

    dma = pltpu.SemaphoreType.DMA
    half = arr(BF16, 2, N_HALF, N_SEC, BLK, HD)

    image, me, gates, tiles, layer = lax.optimization_barrier((image, me, gates, tiles, layer))
    passed = lax.ppermute(image, "section", across)
    give = load(give_kernel, half, [dma((2, N_HALF))], me, wk, wv)
    peer = send(give, partner)
    passed, give = lax.optimization_barrier((passed, give))
    flat = pl.pallas_call(
        pair_kernel,
        name="pair",
        out_shape=arr(BF16, N_SEC // 2, 2, IMG, BLK),
        in_specs=[SMEM_SPEC, VMEM_SPEC, VMEM_SPEC],
        out_specs=VMEM_SPEC,
        compiler_params=pltpu.CompilerParams(vmem_limit_bytes=VMEM_GRANT),
    )(layer, image, pltpu.with_memory_space_constraint(passed, pltpu.VMEM))
    mine = lax.all_to_all(flat, "section", 0, 0, axis_index_groups=groups).reshape(N_SEC, IMG, BLK)
    img_opposite = send(mine, opposite)
    img_first = send(mine, first)
    img_second = send(mine, second)
    wk, wv, text, upstream, mine = lax.optimization_barrier((wk, wv, text, upstream, mine))
    own, text, upstream = load(
        load_kernel, (half, arr(BF16, *text.shape), arr(BF16, *upstream.shape)),
        [dma((2, N_HALF)), dma, dma], me, wk, wv, text, upstream,
    )
    early = call(project_early_kernel, arr(F32, IMG, 4 * HD), 1 << 29, mine, img_opposite, own, peer)
    img_first, img_second, early = lax.optimization_barrier((img_first, img_second, early))
    part, out_part = call(
        project_kernel, (arr(F32, IMG, 2 * HD),) * 2, 1 << 29, early, img_first, img_second, own, peer
    )
    got_part = send(out_part, partner)

    probs, d_scores, rows, grads = call(
        attention_kernel,
        (arr(BF16, GROUP, IMG, TXT), arr(BF16, GROUP, IMG, TXT), arr(BF16, IMG, 2 * HD), arr(BF16, IMG, 2 * HD)),
        1 << 30, tiles, gates, part, got_part, text, upstream,
    )
    others = send(grads, partner)

    def terms(slot, dtype):
        return call(
            functools.partial(term_kernel, slot), arr(dtype, N_SEC, BLK, IMG), 1 << 28, own, peer, grads, others
        )

    got_opposite = send(terms(3, BF16), opposite)
    got_first = send(terms(1, BF16), first)
    got_second = send(terms(2, BF16), second)
    keep = call(term_add_kernel, arr(F32, N_SEC, BLK, IMG), 1 << 28, own, peer, grads, others, got_opposite)
    attended = outside(attended_kernel, gates, probs, rows)
    d_query = outside(dquery_kernel, d_scores, rows)
    got_first, got_second, keep, attended, d_query = lax.optimization_barrier(
        (got_first, got_second, keep, attended, d_query)
    )
    total = call(join_kernel, arr(BF16, N_SEC // 2, 2, BLK, IMG), 1 << 20, keep, got_first, got_second)
    pieces = lax.all_to_all(total, "section", 0, 0, axis_index_groups=groups)
    stay, leave = call(
        half_kernel, (arr(F32, BLK, IMG), arr(BF16, BLK, IMG)), 1 << 20,
        layer, pieces,
    )
    grad = (stay + lax.ppermute(leave, "section", across).astype(F32)).astype(BF16)
    return (attended[None], d_query[None], grad)


def solution(mesh):
    return jax.shard_map(
        shards,
        mesh=mesh,
        in_specs=(
            P("section", "dp", "tensor"),
            P(("section", "tensor"), "dp"),
            P("section", None, "tensor"),
            P("section", None, "tensor"),
            P("section"),
            P("dp"),
            P("section", "dp", "tensor"),
        ),
        out_specs=(
            P("section", "dp", "tensor"),
            P("section", "dp", "tensor"),
            P(("section", "tensor"), "dp"),
        ),
        check_vma=False,
    )
```
